32 devices in a mesh: row: 4 (over y, x), col: 8 (over z, core).
Axes of the slice: x: 2, y: 2, z: 4, core: 2. Of those that a mesh axis runs over, the one named last changes fastest.
Arguments:
- perturbations: float32 [512, 4096], P('row', 'col'), may hold values from -200 to 200
- probes: float32 [4096, 128], P(('col', 'row')), may hold values from -6 to 6
Outputs:
- localized: float32 [4096, 2048], P('col', 'row')
- sampled: float32 [4096, 128], P(('col', 'row'))
The draws below stay inside these ranges and needn't reach their ends.
All inputs are finite; a program needn't handle non-finite values.
Results may differ from the reference program's by a relative error of at most 0.00013.
Values sent between devices are 32-bit elements; how exact they have to be, the bound alone decides.
No kernel may reach another device: no remote copies, remote signals or barrier semaphores. Data moves between devices by JAX's collectives and lax.ppermute only.
A program may use at most 128 MiB of HBM per device.

```python
import math
import jax
import jax.numpy as jnp
from jax import lax

MEMBERS = 512
PROBES = 128
STEPS = 3
STATES = 4096
WINDOW = 1024
N_COL = 8


def draw_perturbations(key, part):
    subkeys = jax.random.split(jax.random.fold_in(key, 17), 6)
    member_noise = jax.random.normal(subkeys[0], (MEMBERS, STATES), jnp.float32)
    state_scale = jnp.exp(jax.random.uniform(subkeys[1], (STATES,), jnp.float32, 0.0, math.log(10.0)))
    member_scale = jnp.exp(jax.random.uniform(subkeys[2], (MEMBERS, 1), jnp.float32, 0.0, math.log(4.0)))
    offsets = 2.0 * jax.random.normal(subkeys[3], (STATES,), jnp.float32)
    factor = jax.random.normal(subkeys[4], (MEMBERS, 1), jnp.float32)
    loading = 0.3 * jax.random.normal(subkeys[5], (STATES,), jnp.float32)
    values = state_scale * (offsets + member_scale * member_noise + factor * loading)
    return jnp.clip(values, -200.0, 200.0)


def level_of(own_key, extent, cuts, low, largest):
    factor_of = 1.0
    for axis_at, blocks in cuts:
        draws = jax.random.uniform(jax.random.fold_in(jax.random.fold_in(own_key, 6), axis_at), (blocks,), jnp.float32, low / len(cuts), largest / len(cuts))
        factor_of = factor_of * jnp.repeat(jnp.exp(draws), extent[axis_at] // blocks).reshape((-1,) + (1,) * (len(extent) - 1 - axis_at))
    return factor_of


def noise(key, shape, deviation, reach, cuts=(), kind=jnp.bfloat16):
    values = jax.random.normal(key, shape, jnp.float32) * deviation
    if len(cuts) > 0:
        values = level_of(key, shape, cuts, -0.22, 0.18) * values
    return jnp.clip(values, min=-reach, max=reach).astype(kind)


def setup_inputs(seed: int = 0) -> dict:
    streams_of = jax.random.split(jax.random.key(seed), 3)
    perturbations = draw_perturbations(jax.random.fold_in(streams_of[2], 71), 0)
    probes = noise(streams_of[1], (STATES, PROBES), 1.0, 6.0, ((0, 32),), jnp.float32)
    return dict(perturbations=perturbations, probes=probes)


epsilon = 1e-06
power_terms = (2.0 / math.pi - 4.0 / (3.0 * math.pi) - 4.0 / (15.0 * math.pi) - 4.0 / (35.0 * math.pi), 8.0 / (3.0 * math.pi) + 32.0 / (15.0 * math.pi) + 72.0 / (35.0 * math.pi), -32.0 / (15.0 * math.pi) - 192.0 / (35.0 * math.pi), 128.0 / (35.0 * math.pi))

def skew_rows(block, width):
    height = block.shape[0]
    length = block.shape[1]
    flattened = jnp.concatenate([block.reshape(-1), jnp.zeros((height,), block.dtype)])
    return flattened.reshape(height, length + 1)[:, :width]

def unskew_rows(band_rows):
    height = band_rows.shape[0]
    width = band_rows.shape[1]
    length = height + width
    padded = jnp.pad(band_rows, ((0, 0), (0, length + 1 - width)))
    return padded.reshape(-1)[:height * length].reshape(height, length)

def reference(perturbations, probes):
    member_mean = lax.optimization_barrier(jnp.sum(perturbations, 0)) / MEMBERS
    centered = perturbations - member_mean
    spread = jnp.sqrt(lax.optimization_barrier(jnp.sum(centered * centered, 0)) + epsilon)
    normed = centered / spread
    block_rows = STATES // N_COL
    extended = jnp.concatenate([normed[:, STATES - WINDOW:], normed, normed[:, :WINDOW]], 1)
    offsets = jnp.arange(2 * WINDOW, dtype=jnp.int32)
    taper = jnp.maximum(jnp.float32(0.0), 1.0 - jnp.abs(offsets - WINDOW).astype(jnp.float32) / WINDOW)

    def one_block(begin_row):
        row_panel = lax.dynamic_slice_in_dim(normed, begin_row, block_rows, 1)
        col_panel = lax.dynamic_slice_in_dim(extended, begin_row, block_rows + 2 * WINDOW, 1)
        gram_block = jnp.dot(row_panel.T, col_panel, precision=lax.Precision.HIGHEST, preferred_element_type=jnp.float32)
        return skew_rows(gram_block, 2 * WINDOW) * taper
    starts = jnp.arange(N_COL, dtype=jnp.int32) * block_rows
    localized = lax.map(one_block, starts).reshape(STATES, 2 * WINDOW)
    scale_norm = jnp.sum(localized * localized) / STATES

    def apply_band(vector):
        vector_ext = jnp.concatenate([vector[STATES - WINDOW:], vector, vector[:WINDOW]], 0)

        def one_product(begin_row):
            band_rows = lax.dynamic_slice_in_dim(localized, begin_row, block_rows, 0)
            window_rows = lax.dynamic_slice_in_dim(vector_ext, begin_row, block_rows + 2 * WINDOW, 0)
            return jnp.dot(unskew_rows(band_rows), window_rows, precision=lax.Precision.HIGHEST, preferred_element_type=jnp.float32)
        return lax.map(one_product, starts).reshape(STATES, PROBES)
    vector = probes
    summed_terms = power_terms[0] * probes
    for power in range(1, STEPS + 1):
        vector = apply_band(vector) / scale_norm
        summed_terms = summed_terms + power_terms[power] * vector
    sampled = jnp.sqrt(scale_norm) * summed_terms
    return (localized, sampled)
```

```python
import functools
import math

import jax
import jax.numpy as jnp
from jax import lax
from jax.experimental import pallas as pl
from jax.experimental.pallas import tpu as pltpu
from jax.sharding import PartitionSpec as P

EPSILON = 1e-06
POWER_TERMS = (
    2.0 / math.pi - 4.0 / (3.0 * math.pi) - 4.0 / (15.0 * math.pi) - 4.0 / (35.0 * math.pi),
    8.0 / (3.0 * math.pi) + 32.0 / (15.0 * math.pi) + 72.0 / (35.0 * math.pi),
    -32.0 / (15.0 * math.pi) - 192.0 / (35.0 * math.pi),
    128.0 / (35.0 * math.pi),
)
EXTRA_ROWS = 8
VMEM = pl.BlockSpec(memory_space=pltpu.VMEM)
SMEM = pl.BlockSpec(memory_space=pltpu.SMEM)
ANY = pl.BlockSpec(memory_space=pl.ANY)
NN = (((1,), (0,)), ((), ()))
NT = (((1,), (1,)), ((), ()))


def col_shift(block, step):
    count = lax.axis_size("col")
    return lax.ppermute(block, "col", [((i + step) % count, i) for i in range(count)])


def core_swap(block):
    return lax.ppermute(block, "col", [(i ^ 1, i) for i in range(lax.axis_size("col"))])


def row_xor(block, mask):
    return lax.ppermute(block, "row", [(i ^ mask, i) for i in range(lax.axis_size("row"))])


def split(value):
    high = value.astype(jnp.bfloat16)
    return high, (value - high.astype(jnp.float32)).astype(jnp.bfloat16)


def dot(a, b, dims):
    return lax.dot_general(a, b, dims, preferred_element_type=jnp.float32)


def normalize(pieces):
    members = sum(p.shape[0] for p in pieces)
    x = jnp.concatenate([p[...] for p in pieces], 0)
    centered = x - jnp.sum(x, 0, keepdims=True) / members
    spread = jnp.sqrt(jnp.sum(centered * centered, 0, keepdims=True) + EPSILON)
    return centered * (1.0 / spread)


def gram_block(offset, left_high, left_low, normed, high_ref, low_ref, square_ref, window):
    n = normed.shape[1]
    high, low = split(normed)
    part = dot(left_high, high, NN) + dot(left_high, low, NN) + dot(left_low, high, NN)
    ahead = lax.broadcasted_iota(jnp.int32, (n, n), 1) - lax.broadcasted_iota(jnp.int32, (n, n), 0)
    distance = jnp.abs(ahead + offset * n).astype(jnp.float32)
    tapered = part * jnp.maximum(0.0, 1.0 - distance * (1.0 / window))
    high, low = split(tapered)
    high_ref[...] = high
    low_ref[...] = low
    square_ref[...] = jnp.sum((tapered * tapered).reshape(n // 8, 8, n), 0)


def own_kernel(count, window, *refs):
    pieces = refs[:count]
    left_high_ref, left_low_ref, high_ref, low_ref, square_ref = refs[count:]
    normed = normalize(pieces)
    left_high, left_low = split(normed.T)
    left_high_ref[...] = left_high
    left_low_ref[...] = left_low
    gram_block(0, left_high, left_low, normed, high_ref, low_ref, square_ref, window)


def other_kernel(count, window, *refs):
    offset_ref, left_high_ref, left_low_ref = refs[:3]
    pieces = refs[3 : 3 + count]
    high_ref, low_ref, square_ref = refs[3 + count :]
    gram_block(
        offset_ref[0], left_high_ref[...], left_low_ref[...], normalize(pieces),
        high_ref, low_ref, square_ref, window,
    )


def own_gram(pieces, window):
    n = pieces[0].shape[1]
    members = sum(p.shape[0] for p in pieces)
    left = jax.ShapeDtypeStruct((n, members), jnp.bfloat16)
    band = jax.ShapeDtypeStruct((n, n), jnp.bfloat16)
    return pl.pallas_call(
        functools.partial(own_kernel, len(pieces), window),
        out_shape=(left, left, band, band, jax.ShapeDtypeStruct((8, n), jnp.float32)),
        in_specs=[VMEM] * len(pieces),
        out_specs=[VMEM] * 5,
        name="own_gram",
        cost_estimate=pl.CostEstimate(flops=6 * n * n * members, bytes_accessed=4 * n * members, transcendentals=0),
    )(*pieces)


def other_gram(offset, left, pieces, window):
    n = pieces[0].shape[1]
    members = sum(p.shape[0] for p in pieces)
    band = jax.ShapeDtypeStruct((n, n), jnp.bfloat16)
    return pl.pallas_call(
        functools.partial(other_kernel, len(pieces), window),
        out_shape=(band, band, jax.ShapeDtypeStruct((8, n), jnp.float32)),
        in_specs=[SMEM] + [VMEM] * (2 + len(pieces)),
        out_specs=[VMEM] * 3,
        name="other_gram",
        cost_estimate=pl.CostEstimate(flops=6 * n * n * members, bytes_accessed=4 * n * members, transcendentals=0),
    )(offset, *left, *pieces)


def band_product(bands, windows, probes):
    n = bands[0][0].shape[0]
    wide = jnp.zeros((2 * probes, n), jnp.float32)
    narrow = jnp.zeros((probes, n), jnp.float32)
    for (high_ref, low_ref), w_ref in zip(bands, windows):
        high, low = split(w_ref[:probes, :])
        band_high = high_ref[...]
        wide += dot(jnp.concatenate([high, low], 0), band_high, NT)
        narrow += dot(high, low_ref[...], NT)
    return wide[:probes] + wide[probes:] + narrow


def unpack(refs, slots):
    bands = list(zip(refs[:slots], refs[slots : 2 * slots]))
    return bands, refs[2 * slots : 3 * slots], refs[3 * slots :]


def first_kernel(slots, probes, *refs):
    bands, windows, rest = unpack(refs, slots)
    squares, y_ref = rest[:slots], rest[slots]
    n = y_ref.shape[1]
    total = squares[0][...]
    for square in squares[1:]:
        total += square[...]
    y_ref[:probes, :] = band_product(bands, windows, probes)
    y_ref[probes:, :] = jnp.broadcast_to(jnp.sum(jnp.sum(total, 1, keepdims=True), 0, keepdims=True), (EXTRA_ROWS, n))


def second_kernel(slots, probes, reach_pairs, *refs):
    bands, windows, (y_ref,) = unpack(refs, slots)
    y_ref[:probes, :] = band_product(bands, windows, probes)
    here = [windows[k][probes : probes + 1, :] for k in range(2 * reach_pairs + 1)]
    y_ref[probes : probes + 1, :] = functools.reduce(jnp.add, here)
    y_ref[probes + 1 : probes + 2, :] = functools.reduce(jnp.add, here[reach_pairs + 1 :])
    behind = here[1:reach_pairs]
    y_ref[probes + 2 : probes + 3, :] = functools.reduce(jnp.add, behind) if behind else jnp.zeros_like(here[0])
    y_ref[probes + 3 :, :] = jnp.zeros((EXTRA_ROWS - 3, y_ref.shape[1]), jnp.float32)


def last_kernel(slots, probes, state_count, *refs):
    bands, windows, (w0_ref, y1_ref, y2_ref, sum_ref, out_ref) = unpack(refs, slots)
    y3 = band_product(bands, windows, probes)
    scale = sum_ref[...] / state_count
    total = POWER_TERMS[0] * w0_ref[...]
    total += POWER_TERMS[1] * (y1_ref[:probes, :] / scale)
    total += POWER_TERMS[2] * (y2_ref[:probes, :] / scale / scale)
    total += POWER_TERMS[3] * (y3 / scale / scale / scale)
    out_ref[...] = jnp.sqrt(scale) * total


def skew_kernel(slots, *refs):
    picks_ref, out_ref = refs[0], refs[1 + 2 * slots]
    high_scratch, low_scratch, sem = refs[2 + 2 * slots :]
    n = out_ref.shape[0]
    for place in range(2):
        for k in range(slots):
            @pl.when(picks_ref[place] == k)
            def _(place=place, k=k):
                a = pltpu.make_async_copy(refs[1 + k], high_scratch.at[place], sem.at[0])
                b = pltpu.make_async_copy(refs[1 + slots + k], low_scratch.at[place], sem.at[1])
                a.start()
                b.start()
                a.wait()
                b.wait()

    group = 16

    def body(g, carry):
        start = pl.multiple_of(g * group, group)
        rows = pl.ds(start, group)
        near = high_scratch[0, rows, :].astype(jnp.float32) + low_scratch[0, rows, :].astype(jnp.float32)
        far = high_scratch[1, rows, :].astype(jnp.float32) + low_scratch[1, rows, :].astype(jnp.float32)
        row = lax.broadcasted_iota(jnp.int32, (group, n), 0)
        lane = lax.broadcasted_iota(jnp.int32, (group, n), 1)
        value = jnp.where(lane >= row + start, near, far)
        value = pltpu.roll(value, lax.rem(n - start, n), 1)
        bit = 1
        while bit < group:
            value = jnp.where((row & bit) != 0, pltpu.roll(value, n - bit, 1), value)
            bit *= 2
        out_ref[rows, :] = value
        return carry

    lax.fori_loop(0, n // group, body, 0)


def skewed(picks, bands):
    slots = len(bands)
    n = bands[0][0].shape[0]
    return pl.pallas_call(
        functools.partial(skew_kernel, slots),
        out_shape=jax.ShapeDtypeStruct((n, n), jnp.float32),
        in_specs=[SMEM] + [ANY] * (2 * slots),
        out_specs=VMEM,
        scratch_shapes=[
            pltpu.VMEM((2, n, n), jnp.bfloat16),
            pltpu.VMEM((2, n, n), jnp.bfloat16),
            pltpu.SemaphoreType.DMA((2,)),
        ],
        name="skew_out",
        cost_estimate=pl.CostEstimate(flops=40 * n * n, bytes_accessed=12 * n * n, transcendentals=0),
    )(picks, *[b[0] for b in bands], *[b[1] for b in bands])


def step_call(kernel, name, bands, windows, extra, rows):
    n = bands[0][0].shape[0]
    operands = [b[0] for b in bands] + [b[1] for b in bands] + list(windows) + list(extra)
    return pl.pallas_call(
        kernel,
        out_shape=jax.ShapeDtypeStruct((rows, n), jnp.float32),
        in_specs=[VMEM] * len(operands),
        out_specs=VMEM,
        name=name,
        cost_estimate=pl.CostEstimate(flops=6 * n * n * rows * len(bands), bytes_accessed=4 * n * n * len(bands), transcendentals=0),
    )(*operands)


def on_device(perturbations, probes):
    row_count = lax.axis_size("row")
    col_count = lax.axis_size("col")
    row_index = lax.axis_index("row")
    core = lax.axis_index("col") % 2
    n = perturbations.shape[1]
    state_count = n * col_count
    window = state_count // 4
    reach = col_count // 4
    pairs = reach // 2
    probe_count = probes.shape[1] // row_count
    sides = [t for t in range(-pairs, pairs + 1) if t != 0]

    def window_of(held):
        inner = [core_swap(held[t]) for t in range(1 - pairs, pairs)]
        outer = core_swap(jnp.where(core == 1, held[-pairs], held[pairs]))
        return [held[t] for t in range(-pairs, pairs + 1)] + inner + [outer]

    blocks = {0: [perturbations]}
    for t in sides:
        blocks[t] = [col_shift(perturbations, 2 * t)]
    for mask in range(1, row_count):
        blocks[0].append(row_xor(perturbations, mask))
    for t in sides:
        for mask in range(1, row_count - 1):
            blocks[t].append(row_xor(blocks[t][0], mask))
        blocks[t].append(col_shift(blocks[0][-1], 2 * t))
    stacked = {t: jnp.concatenate(b, 0) for t, b in blocks.items()}
    members = window_of(stacked)

    w0 = lax.all_to_all(probes.T, "row", split_axis=0, concat_axis=1, tiled=True)
    held = {0: w0}
    for t in sides:
        held[t] = col_shift(w0, 2 * t)
    windows = window_of(held)

    partner = 1 - 2 * core
    offsets = [2 * t for t in range(-pairs, pairs + 1)]
    offsets += [2 * t + partner for t in range(1 - pairs, pairs)] + [-partner * (reach - 1)]
    slots = len(offsets)
    bands = [None] * slots
    squares = [None] * slots
    left_high, left_low, high, low, square = own_gram(blocks[0], window)
    bands[pairs], squares[pairs] = (high, low), square
    for k in range(slots):
        if k != pairs:
            pieces = blocks[k - pairs] if k <= 2 * pairs else [members[k]]
            offset = jnp.asarray(offsets[k], jnp.int32).reshape(1)
            high, low, square = other_gram(offset, (left_high, left_low), pieces, window)
            bands[k], squares[k] = (high, low), square

    def slot_of(offset):
        inner = 2 * pairs + 1 + (offset - partner) // 2 + pairs - 1
        odd = jnp.where(offset == -partner * (reach - 1), slots - 1, inner)
        return jnp.where(offset % 2 == 0, offset // 2 + pairs, odd)

    near = row_index - reach
    picks = jnp.stack([slot_of(near), slot_of(near + 1)]).astype(jnp.int32)
    localized = skewed(picks, bands)

    rows = probe_count + EXTRA_ROWS
    y1 = step_call(functools.partial(first_kernel, slots, probe_count), "step_1", bands, windows, squares, rows)
    held = {0: y1}
    for t in sides:
        held[t] = col_shift(y1, 2 * t)
    windows = window_of(held)
    y2 = step_call(functools.partial(second_kernel, slots, probe_count, pairs), "step_2", bands, windows, [], rows)
    held = {0: y2}
    for t in sides:
        held[t] = col_shift(y2, 2 * t)
    same = y2[probe_count] + held[pairs][probe_count + 1] + held[-pairs][probe_count + 2]
    tail = jnp.broadcast_to(same[None], (EXTRA_ROWS, n))
    inner = [core_swap(held[t]) for t in range(1 - pairs, pairs)]
    chosen = jnp.where(core == 1, held[-pairs], held[pairs])
    outer = core_swap(jnp.concatenate([chosen[:probe_count], tail], 0))
    windows = [held[t] for t in range(-pairs, pairs + 1)] + inner + [outer]
    total = (same + outer[probe_count])[None]
    sampled = step_call(
        functools.partial(last_kernel, slots, probe_count, state_count), "step_3", bands, windows, [w0, y1, y2, total], probe_count
    )
    sampled = lax.all_to_all(sampled, "row", split_axis=1, concat_axis=0, tiled=True).T
    return (localized, sampled)


def solution(mesh):
    return jax.shard_map(
        on_device,
        mesh=mesh,
        in_specs=(P("row", "col"), P(("col", "row"), None)),
        out_specs=(P("col", "row"), P(("col", "row"), None)),
        check_vma=False,
    )
```

```python
import functools
import math

import jax
import jax.numpy as jnp
from jax import lax
from jax.experimental import pallas as pl
from jax.experimental.pallas import tpu as pltpu
from jax.sharding import PartitionSpec as P


EPSILON = 1e-06
POWER_TERMS = (
    2.0 / math.pi - 4.0 / (3.0 * math.pi) - 4.0 / (15.0 * math.pi) - 4.0 / (35.0 * math.pi),
    8.0 / (3.0 * math.pi) + 32.0 / (15.0 * math.pi) + 72.0 / (35.0 * math.pi),
    -32.0 / (15.0 * math.pi) - 192.0 / (35.0 * math.pi),
    128.0 / (35.0 * math.pi),
)
EXTRA_ROWS = 8
VMEM = pl.BlockSpec(memory_space=pltpu.VMEM)
SMEM = pl.BlockSpec(memory_space=pltpu.SMEM)
ANY = pl.BlockSpec(memory_space=pl.ANY)
NN = (((1,), (0,)), ((), ()))
NT = (((1,), (1,)), ((), ()))


def col_shift(block, step):
    count = lax.axis_size("col")
    return lax.ppermute(block, "col", [((i + step) % count, i) for i in range(count)])


def core_swap(block):
    return lax.ppermute(block, "col", [(i ^ 1, i) for i in range(lax.axis_size("col"))])


def row_xor(block, mask):
    return lax.ppermute(block, "row", [(i ^ mask, i) for i in range(lax.axis_size("row"))])


def vmem_limit(*arrays, scratch=0):
    held = sum(math.prod(a.shape) * a.dtype.itemsize for a in arrays) + scratch
    return pltpu.CompilerParams(vmem_limit_bytes=min(held + (4 << 20), 60 << 20))


def split(value):
    high = value.astype(jnp.bfloat16)
    return high, (value - high.astype(jnp.float32)).astype(jnp.bfloat16)


def dot(a, b, dims):
    return lax.dot_general(a, b, dims, preferred_element_type=jnp.float32)


def normalize(pieces):
    members = sum(p.shape[0] for p in pieces)
    x = jnp.concatenate([p[...] for p in pieces], 0)
    centered = x - jnp.sum(x, 0, keepdims=True) / members
    spread = jnp.sqrt(jnp.sum(centered * centered, 0, keepdims=True) + EPSILON)
    return centered * (1.0 / spread)


def gram_block(offset, left_high, left_low, normed, high_ref, low_ref, square_ref, window):
    n = normed.shape[1]
    high, low = split(normed)
    part = dot(left_high, high, NN) + dot(left_high, low, NN) + dot(left_low, high, NN)
    ahead = lax.broadcasted_iota(jnp.int32, (n, n), 1) - lax.broadcasted_iota(jnp.int32, (n, n), 0)
    distance = jnp.abs(ahead + offset * n).astype(jnp.float32)
    tapered = part * jnp.maximum(0.0, 1.0 - distance * (1.0 / window))
    high, low = split(tapered)
    high_ref[...] = high
    low_ref[...] = low
    square_ref[...] = jnp.sum((tapered * tapered).reshape(n // 8, 8, n), 0)


def own_kernel(count, window, *refs):
    pieces = refs[:count]
    left_high_ref, left_low_ref, high_ref, low_ref, square_ref, normed_ref = refs[count:]
    normed = normalize(pieces)
    normed_ref[...] = normed
    left_high, left_low = split(normed.T)
    left_high_ref[...] = left_high
    left_low_ref[...] = left_low
    gram_block(0, left_high, left_low, normed, high_ref, low_ref, square_ref, window)


def other_kernel(count, window, raw, *refs):
    offset_ref, left_high_ref, left_low_ref = refs[:3]
    pieces = refs[3 : 3 + count]
    high_ref, low_ref, square_ref = refs[3 + count :]
    normed = normalize(pieces) if raw else pieces[0][...]
    gram_block(
        offset_ref[0], left_high_ref[...], left_low_ref[...], normed,
        high_ref, low_ref, square_ref, window,
    )


def own_gram(pieces, window):
    n = pieces[0].shape[1]
    members = sum(p.shape[0] for p in pieces)
    left = jax.ShapeDtypeStruct((n, members), jnp.bfloat16)
    band = jax.ShapeDtypeStruct((n, n), jnp.bfloat16)
    outs = (left, left, band, band, jax.ShapeDtypeStruct((8, n), jnp.float32), jax.ShapeDtypeStruct((members, n), jnp.float32))
    return pl.pallas_call(
        functools.partial(own_kernel, len(pieces), window),
        out_shape=outs,
        compiler_params=vmem_limit(*pieces, *outs, scratch=16 * n * (n + members)),
        in_specs=[VMEM] * len(pieces),
        out_specs=[VMEM] * 6,
        name="own_gram",
        cost_estimate=pl.CostEstimate(flops=6 * n * n * members, bytes_accessed=4 * n * members, transcendentals=0),
    )(*pieces)


def other_gram(offset, left, pieces, window, raw=True):
    n = pieces[0].shape[1]
    members = sum(p.shape[0] for p in pieces)
    band = jax.ShapeDtypeStruct((n, n), jnp.bfloat16)
    outs = (band, band, jax.ShapeDtypeStruct((8, n), jnp.float32))
    return pl.pallas_call(
        functools.partial(other_kernel, len(pieces), window, raw),
        out_shape=outs,
        compiler_params=vmem_limit(*left, *pieces, *outs, scratch=16 * n * (n + members)),
        in_specs=[SMEM] + [VMEM] * (2 + len(pieces)),
        out_specs=[VMEM] * 3,
        cost_estimate=pl.CostEstimate(flops=6 * n * n * members, bytes_accessed=4 * n * members, transcendentals=0),
    )(offset, *left, *pieces)


def band_product(bands, windows, probes):
    n = bands[0][0].shape[0]
    wide = jnp.zeros((2 * probes, n), jnp.float32)
    narrow = jnp.zeros((probes, n), jnp.float32)
    for (high_ref, low_ref), w_ref in zip(bands, windows):
        high, low = split(w_ref[:probes, :])
        band_high = high_ref[...]
        wide += dot(jnp.concatenate([high, low], 0), band_high, NT)
        narrow += dot(high, low_ref[...], NT)
    return wide[:probes] + wide[probes:] + narrow


def unpack(refs, slots):
    bands = list(zip(refs[:slots], refs[slots : 2 * slots]))
    return bands, refs[2 * slots : 3 * slots], refs[3 * slots :]


def first_kernel(slots, probes, *refs):
    bands, windows, rest = unpack(refs, slots)
    squares, y_ref = rest[:slots], rest[slots]
    n = y_ref.shape[1]
    total = squares[0][...]
    for square in squares[1:]:
        total += square[...]
    y_ref[:probes, :] = band_product(bands, windows, probes)
    y_ref[probes:, :] = jnp.broadcast_to(jnp.sum(jnp.sum(total, 1, keepdims=True), 0, keepdims=True), (EXTRA_ROWS, n))


def second_kernel(slots, probes, reach_pairs, *refs):
    bands, windows, (y_ref,) = unpack(refs, slots)
    y_ref[:probes, :] = band_product(bands, windows, probes)
    here = [windows[k][probes : probes + 1, :] for k in range(2 * reach_pairs + 1)]
    zero = jnp.zeros_like(here[0])
    y_ref[probes : probes + 1, :] = functools.reduce(jnp.add, here)
    y_ref[probes + 1 : probes + 2, :] = functools.reduce(jnp.add, here[reach_pairs + 1 :], zero)
    y_ref[probes + 2 : probes + 3, :] = functools.reduce(jnp.add, here[1:reach_pairs], zero)
    y_ref[probes + 3 :, :] = jnp.zeros((EXTRA_ROWS - 3, y_ref.shape[1]), jnp.float32)


def last_kernel(slots, probes, reach_pairs, state_count, *refs):
    bands, windows, (w0_ref, y1_ref, y2_ref, out_ref) = unpack(refs, slots)
    y3 = band_product(bands, windows, probes)
    sums = y2_ref[probes : probes + 1, :] + windows[2 * reach_pairs][probes + 1 : probes + 2, :]
    sums += windows[0][probes + 2 : probes + 3, :]
    for row in range(probes, probes + 3):
        sums += windows[-1][row : row + 1, :]
    scale = sums / state_count
    total = POWER_TERMS[0] * w0_ref[...]
    total += POWER_TERMS[1] * (y1_ref[:probes, :] / scale)
    total += POWER_TERMS[2] * (y2_ref[:probes, :] / scale / scale)
    total += POWER_TERMS[3] * (y3 / scale / scale / scale)
    out_ref[...] = jnp.sqrt(scale) * total


def skew_kernel(slots, *refs):
    picks_ref, out_ref = refs[0], refs[1 + 2 * slots]
    high_scratch, low_scratch, sem = refs[2 + 2 * slots :]
    n = out_ref.shape[0]
    for place in range(2):
        for k in range(slots):
            @pl.when(picks_ref[place] == k)
            def _(place=place, k=k):
                a = pltpu.make_async_copy(refs[1 + k], high_scratch.at[place], sem.at[0])
                b = pltpu.make_async_copy(refs[1 + slots + k], low_scratch.at[place], sem.at[1])
                a.start()
                b.start()
                a.wait()
                b.wait()

    group = 8
    flip = group - 1 - lax.broadcasted_iota(jnp.int32, (group, n), 0)
    row = lax.broadcasted_iota(jnp.int32, (2 * group, n), 0)
    lane = lax.broadcasted_iota(jnp.int32, (2 * group, n), 1)
    for start in range(0, n, 2 * group):
        rows = slice(start, start + 2 * group)
        near = high_scratch[0, rows, :].astype(jnp.float32) + low_scratch[0, rows, :].astype(jnp.float32)
        far = high_scratch[1, rows, :].astype(jnp.float32) + low_scratch[1, rows, :].astype(jnp.float32)
        value = jnp.where(lane >= row + start, near, far)
        for half in (0, group):
            part = jnp.take_along_axis(value[half : half + group], flip, axis=0)
            part = pltpu.roll(part, (2 * n - start - half - group + 1) % n, 1, stride=1, stride_axis=0)
            out_ref[start + half : start + half + group, :] = jnp.take_along_axis(part, flip, axis=0)


def skewed(picks, bands):
    slots = len(bands)
    n = bands[0][0].shape[0]
    return pl.pallas_call(
        functools.partial(skew_kernel, slots),
        out_shape=jax.ShapeDtypeStruct((n, n), jnp.float32),
        in_specs=[SMEM] + [ANY] * (2 * slots),
        out_specs=VMEM,
        compiler_params=vmem_limit(scratch=12 * n * n),
        scratch_shapes=[
            pltpu.VMEM((2, n, n), jnp.bfloat16),
            pltpu.VMEM((2, n, n), jnp.bfloat16),
            pltpu.SemaphoreType.DMA((2,)),
        ],
        name="skew_out",
        cost_estimate=pl.CostEstimate(flops=40 * n * n, bytes_accessed=12 * n * n, transcendentals=0),
    )(picks, *[b[0] for b in bands], *[b[1] for b in bands])


def step_call(kernel, bands, windows, extra, rows):
    n = bands[0][0].shape[0]
    operands = [b[0] for b in bands] + [b[1] for b in bands] + list(windows) + list(extra)
    return pl.pallas_call(
        kernel,
        out_shape=jax.ShapeDtypeStruct((rows, n), jnp.float32),
        compiler_params=vmem_limit(*operands, scratch=32 * rows * n),
        in_specs=[VMEM] * len(operands),
        out_specs=VMEM,
        cost_estimate=pl.CostEstimate(flops=6 * n * n * rows * len(bands), bytes_accessed=4 * n * n * len(bands), transcendentals=0),
    )(*operands)


def on_device(perturbations, probes):
    row_count = lax.axis_size("row")
    col_count = lax.axis_size("col")
    row_index = lax.axis_index("row")
    core = lax.axis_index("col") % 2
    n = perturbations.shape[1]
    state_count = n * col_count
    window = state_count // 4
    reach = col_count // 4
    pairs = reach // 2
    probe_count = probes.shape[1] // row_count
    sides = [t for t in range(-pairs, pairs + 1) if t != 0]

    def window_of(held, outer):
        inner = [core_swap(held[t]) for t in range(1 - pairs, pairs)]
        return [held[t] for t in range(-pairs, pairs + 1)] + inner + [core_swap(outer)]

    def far_pick(held):
        return jnp.where(core == 1, held[-pairs], held[pairs])

    def exchange(block):
        return {0: block} | {t: col_shift(block, 2 * t) for t in sides}

    last_mask = row_count - 1
    blocks = {0: {0: perturbations}}
    for t in sides:
        blocks[t] = {0: col_shift(perturbations, 2 * t)}
    for mask in range(last_mask, 0, -1):
        blocks[0][mask] = row_xor(perturbations, mask)
    w0 = lax.all_to_all(probes.T, "row", split_axis=0, concat_axis=1, tiled=True)
    held = exchange(w0)
    windows = window_of(held, far_pick(held))
    for t in sides:
        for mask in range(1, last_mask):
            blocks[t][mask] = row_xor(blocks[t][0], mask)
        blocks[t][last_mask] = col_shift(blocks[0][last_mask], 2 * t)

    partner = 1 - 2 * core
    offsets = [2 * t for t in range(-pairs, pairs + 1)]
    offsets += [2 * t + partner for t in range(1 - pairs, pairs)] + [-partner * (reach - 1)]
    slots = len(offsets)
    bands = {}
    squares = {}
    left_high, left_low, high, low, square, normed = own_gram([blocks[0][k] for k in range(row_count)], window)
    left = (left_high, left_low)
    bands[pairs], squares[pairs] = (high, low), square

    def add_slot(k, pieces, raw=True):
        offset = jnp.asarray(offsets[k], jnp.int32).reshape(1)
        high, low, square = other_gram(offset, left, pieces, window, raw)
        bands[k], squares[k] = (high, low), square

    for t in range(1 - pairs, pairs):
        if t == 0:
            add_slot(3 * pairs, [core_swap(normed)], raw=False)
        else:
            pieces = [core_swap(blocks[t][k]) for k in range(row_count)]
            add_slot(3 * pairs + t, pieces)
    far = [core_swap(far_pick({t: blocks[t][k] for t in sides})) for k in range(row_count)]
    for t in sides:
        add_slot(pairs + t, [blocks[t][k] for k in range(row_count)])
    add_slot(slots - 1, far)
    bands = [bands[k] for k in range(slots)]
    squares = [squares[k] for k in range(slots)]

    def slot_of(offset):
        inner = 3 * pairs + (offset - partner) // 2
        odd = jnp.where(offset == -partner * (reach - 1), slots - 1, inner)
        return jnp.where(offset % 2 == 0, offset // 2 + pairs, odd)

    near = row_index - reach
    picks = jnp.stack([slot_of(near), slot_of(near + 1)]).astype(jnp.int32)
    localized = skewed(picks, bands)

    rows = probe_count + EXTRA_ROWS
    y1 = step_call(functools.partial(first_kernel, slots, probe_count), bands, windows, squares, rows)
    held = exchange(y1)
    windows = window_of(held, far_pick(held))
    y2 = step_call(functools.partial(second_kernel, slots, probe_count, pairs), bands, windows, [], rows)
    held = exchange(y2)
    row = lax.broadcasted_iota(jnp.int32, y2.shape, 0) - probe_count
    tail = jnp.where(row == 0, y2, jnp.where(row == 1, held[pairs], held[-pairs]))
    windows = window_of(held, jnp.where(row < 0, far_pick(held), tail))
    sampled = step_call(
        functools.partial(last_kernel, slots, probe_count, pairs, state_count), bands, windows, [w0, y1, y2], probe_count
    )
    sampled = lax.all_to_all(sampled, "row", split_axis=1, concat_axis=0, tiled=True).T
    return (localized, sampled)


def solution(mesh):
    return jax.shard_map(
        on_device,
        mesh=mesh,
        in_specs=(P("row", "col"), P(("col", "row"), None)),
        out_specs=(P("col", "row"), P(("col", "row"), None)),
        check_vma=False,
    )
```

```python
import functools
import math

import jax
import jax.numpy as jnp
from jax import lax
from jax.experimental import pallas as pl
from jax.experimental.pallas import tpu as pltpu
from jax.sharding import PartitionSpec as P


EPSILON = 1e-06
POWER_TERMS = (
    2.0 / math.pi - 4.0 / (3.0 * math.pi) - 4.0 / (15.0 * math.pi) - 4.0 / (35.0 * math.pi),
    8.0 / (3.0 * math.pi) + 32.0 / (15.0 * math.pi) + 72.0 / (35.0 * math.pi),
    -32.0 / (15.0 * math.pi) - 192.0 / (35.0 * math.pi),
    128.0 / (35.0 * math.pi),
)
EXTRA_ROWS = 8
VMEM = pl.BlockSpec(memory_space=pltpu.VMEM)
ANY = pl.BlockSpec(memory_space=pl.ANY)
NN = (((1,), (0,)), ((), ()))
NT = (((1,), (1,)), ((), ()))


def side_sign(side):
    span, late = side
    odd = (lax.axis_index("col") // 2 // span) & 1
    return (1 - 2 * late) * (2 * odd - 1)


def ring_swap(block, side):
    span, late = side
    count = lax.axis_size("col") // 2
    route = []
    for i in range(count):
        ahead = (i // span) % 2 != late
        other = (i + span if ahead else i - span) % count
        route += [(2 * i, 2 * other), (2 * i + 1, 2 * other + 1)]
    return lax.ppermute(block, "col", route)


def core_swap(block):
    return lax.ppermute(block, "col", [(i ^ 1, i) for i in range(lax.axis_size("col"))])


def row_xor(block, mask):
    return lax.ppermute(block, "row", [(i ^ mask, i) for i in range(lax.axis_size("row"))])


def vmem_limit(*arrays, scratch=0):
    held = sum(math.prod(a.shape) * a.dtype.itemsize for a in arrays) + scratch
    return pltpu.CompilerParams(vmem_limit_bytes=min(held + (4 << 20), 60 << 20))


def split(value):
    high = value.astype(jnp.bfloat16)
    return high, (value - high.astype(jnp.float32)).astype(jnp.bfloat16)


def dot(a, b, dims):
    return lax.dot_general(a, b, dims, preferred_element_type=jnp.float32)


def normalize(pieces):
    members = sum(p.shape[0] for p in pieces)
    x = jnp.concatenate([p[...] for p in pieces], 0)
    centered = x - jnp.sum(x, 0, keepdims=True) / members
    spread = jnp.sqrt(jnp.sum(centered * centered, 0, keepdims=True) + EPSILON)
    return centered * (1.0 / spread)


def device_core():
    return lax.axis_index("col") & 1


def gram_kernel(window, count, offset, raw, last, *refs):
    refs = list(refs)
    take = lambda k: [refs.pop(0) for _ in range(k)]
    own = offset is None
    left_high_ref, left_low_ref = (None, None) if own else take(2)
    pieces = take(count)
    (w_ref,) = take(1)
    sum_ref, squares_ref = (None, None) if own else take(2)
    high_ref, low_ref, y_ref, square_ref = take(4)
    normed = normalize(pieces) if raw else pieces[0][...]
    n = normed.shape[1]
    if own:
        left_high_out, left_low_out, normed_out = take(3)
        normed_out[...] = normed
        left_high, left_low = split(normed.T)
        left_high_out[...] = left_high
        left_low_out[...] = left_low
    else:
        left_high, left_low = left_high_ref[...], left_low_ref[...]
    high, low = split(normed)
    part = dot(left_high, high, NN) + dot(left_high, low, NN) + dot(left_low, high, NN)
    ahead = lax.broadcasted_iota(jnp.int32, (n, n), 1) - lax.broadcasted_iota(jnp.int32, (n, n), 0)
    shift = 0 if own else offset() * n
    distance = jnp.abs(ahead + shift).astype(jnp.float32)
    tapered = part * jnp.maximum(0.0, 1.0 - distance * (1.0 / window))
    high, low = split(tapered)
    high_ref[...] = high
    low_ref[...] = low
    square = jnp.sum((tapered * tapered).reshape(n // 8, 8, n), 0)
    product = band_product([(high_ref, low_ref)], [w_ref], w_ref.shape[0])
    if not own:
        square += squares_ref[...]
        product += sum_ref[...]
    probes = product.shape[0]
    y_ref[:probes, :] = product
    if last:
        total = jnp.sum(jnp.sum(square, 1, keepdims=True), 0, keepdims=True)
        y_ref[probes:, :] = jnp.broadcast_to(total, (EXTRA_ROWS, n))
    square_ref[...] = square


def gram(offset, left, pieces, w, carried, window, raw=True, last=False):
    own = offset is None
    n = pieces[0].shape[1]
    members = sum(p.shape[0] for p in pieces)
    probes = w.shape[0]
    band = jax.ShapeDtypeStruct((n, n), jnp.bfloat16)
    side = jax.ShapeDtypeStruct((n, members), jnp.bfloat16)
    y = jax.ShapeDtypeStruct((probes + (EXTRA_ROWS if last else 0), n), jnp.float32)
    outs = [band, band, y, jax.ShapeDtypeStruct((8, n), jnp.float32)]
    operands = [*pieces, w]
    if own:
        outs += [side, side, jax.ShapeDtypeStruct((members, n), jnp.float32)]
    else:
        operands = [*left, *operands, *carried]
    specs = [VMEM] * len(operands)
    return pl.pallas_call(
        functools.partial(gram_kernel, window, len(pieces), offset, raw, last),
        out_shape=tuple(outs),
        compiler_params=vmem_limit(*operands, *outs, scratch=16 * n * (n + members)),
        in_specs=specs,
        out_specs=[VMEM] * len(outs),
        cost_estimate=pl.CostEstimate(flops=6 * n * n * members, bytes_accessed=4 * n * members, transcendentals=0),
    )(*operands)


def band_product(bands, windows, probes):
    n = bands[0][0].shape[0]
    wide = jnp.zeros((2 * probes, n), jnp.float32)
    narrow = jnp.zeros((probes, n), jnp.float32)
    for (high_ref, low_ref), w_ref in zip(bands, windows):
        high, low = split(w_ref[:probes, :])
        band_high = high_ref[...]
        wide += dot(jnp.concatenate([high, low], 0), band_high, NT)
        narrow += dot(high, low_ref[...], NT)
    return wide[:probes] + wide[probes:] + narrow


def unpack(refs, slots):
    bands = list(zip(refs[:slots], refs[slots : 2 * slots]))
    return bands, refs[2 * slots : 3 * slots], refs[3 * slots :]


def second_kernel(slots, probes, reach_pairs, *refs):
    bands, windows, (y_ref,) = unpack(refs, slots)
    y_ref[:probes, :] = band_product(bands, windows, probes)
    here = [windows[k][probes : probes + 1, :] for k in range(2 * reach_pairs + 1)]
    ahead = jnp.zeros_like(here[0])
    behind = jnp.zeros_like(here[0])
    for span in range(1, reach_pairs + 1):
        first, second = here[2 * span - 1], here[2 * span]
        flag = side_sign((span, 0)) > 0
        ahead += jnp.where(flag, first, second)
        if span < reach_pairs:
            behind += jnp.where(flag, second, first)
    y_ref[probes : probes + 1, :] = functools.reduce(jnp.add, here)
    y_ref[probes + 1 : probes + 2, :] = ahead
    y_ref[probes + 2 : probes + 3, :] = behind
    y_ref[probes + 3 :, :] = jnp.zeros((EXTRA_ROWS - 3, y_ref.shape[1]), jnp.float32)


def last_kernel(slots, probes, reach_pairs, state_count, *refs):
    bands, windows, (w0_ref, y1_ref, y2_ref, *out_refs, total_ref) = unpack(refs, slots)
    y3 = band_product(bands, windows, probes)
    first, second = windows[2 * reach_pairs - 1], windows[2 * reach_pairs]
    flag = side_sign((reach_pairs, 0)) > 0
    sums = y2_ref[probes : probes + 1, :]
    sums += jnp.where(flag, first[probes + 1 : probes + 2, :], second[probes + 1 : probes + 2, :])
    sums += jnp.where(flag, second[probes + 2 : probes + 3, :], first[probes + 2 : probes + 3, :])
    for row in range(probes, probes + 3):
        sums += windows[-1][row : row + 1, :]
    scale = sums / state_count
    total = POWER_TERMS[0] * w0_ref[...]
    total += POWER_TERMS[1] * (y1_ref[:probes, :] / scale)
    total += POWER_TERMS[2] * (y2_ref[:probes, :] / scale / scale)
    total += POWER_TERMS[3] * (y3 / scale / scale / scale)
    total_ref[...] = jnp.sqrt(scale) * total
    width = out_refs[0].shape[1]
    for mask, out_ref in enumerate(out_refs):
        start = pl.multiple_of((lax.axis_index("row") ^ mask) * width, width)
        out_ref[...] = total_ref[:, pl.ds(start, width)]


def gather_kernel(*refs):
    *piece_refs, out_ref, stack_ref = refs
    height = piece_refs[0].shape[0]
    for mask, piece_ref in enumerate(piece_refs):
        start = pl.multiple_of((lax.axis_index("row") ^ mask) * height, height)
        stack_ref[pl.ds(start, height), :] = piece_ref[...]
    out_ref[...] = stack_ref[...].T


def split_kernel(probes_ref, *refs):
    *piece_refs, stack_ref = refs
    stack_ref[...] = probes_ref[...].T
    height = piece_refs[0].shape[0]
    for mask, piece_ref in enumerate(piece_refs):
        start = pl.multiple_of((lax.axis_index("row") ^ mask) * height, height)
        piece_ref[...] = stack_ref[pl.ds(start, height), :]


def join_kernel(*refs):
    *piece_refs, out_ref = refs
    width = piece_refs[0].shape[1]
    for mask, piece_ref in enumerate(piece_refs):
        start = pl.multiple_of((lax.axis_index("row") ^ mask) * width, width)
        out_ref[:, pl.ds(start, width)] = piece_ref[...]


def small_call(kernel, operands, outs, scratch=()):
    return pl.pallas_call(
        kernel,
        out_shape=outs,
        compiler_params=vmem_limit(*operands, *operands),
        in_specs=[VMEM] * len(operands),
        out_specs=jax.tree.map(lambda _: VMEM, outs),
        scratch_shapes=scratch,
    )(*operands)


def skew_kernel(offsets, reach, *refs):
    slots = len(offsets)
    out_ref = refs[2 * slots]
    high_scratch, low_scratch, sem = refs[1 + 2 * slots :]
    n = out_ref.shape[0]
    for place in range(2):
        wanted = lax.axis_index("row") - reach + place
        for k, offset in enumerate(offsets):
            @pl.when(wanted == offset())
            def _(place=place, k=k):
                a = pltpu.make_async_copy(refs[k], high_scratch.at[place], sem.at[0])
                b = pltpu.make_async_copy(refs[slots + k], low_scratch.at[place], sem.at[1])
                a.start()
                b.start()
                a.wait()
                b.wait()

    group = 8
    flip = group - 1 - lax.broadcasted_iota(jnp.int32, (group, n), 0)
    row = lax.broadcasted_iota(jnp.int32, (2 * group, n), 0)
    lane = lax.broadcasted_iota(jnp.int32, (2 * group, n), 1)
    for start in range(0, n, 2 * group):
        rows = slice(start, start + 2 * group)
        near = high_scratch[0, rows, :].astype(jnp.float32) + low_scratch[0, rows, :].astype(jnp.float32)
        far = high_scratch[1, rows, :].astype(jnp.float32) + low_scratch[1, rows, :].astype(jnp.float32)
        value = jnp.where(lane >= row + start, near, far)
        for half in (0, group):
            part = jnp.take_along_axis(value[half : half + group], flip, axis=0)
            part = pltpu.roll(part, (2 * n - start - half - group + 1) % n, 1, stride=1, stride_axis=0)
            out_ref[start + half : start + half + group, :] = jnp.take_along_axis(part, flip, axis=0)


def skewed(offsets, reach, bands):
    slots = len(bands)
    n = bands[0][0].shape[0]
    return pl.pallas_call(
        functools.partial(skew_kernel, offsets, reach),
        out_shape=jax.ShapeDtypeStruct((n, n), jnp.float32),
        in_specs=[ANY] * (2 * slots),
        out_specs=VMEM,
        compiler_params=vmem_limit(scratch=12 * n * n),
        scratch_shapes=[
            pltpu.VMEM((2, n, n), jnp.bfloat16),
            pltpu.VMEM((2, n, n), jnp.bfloat16),
            pltpu.SemaphoreType.DMA((2,)),
        ],
        name="skew_out",
        cost_estimate=pl.CostEstimate(flops=40 * n * n, bytes_accessed=12 * n * n, transcendentals=0),
    )(*[b[0] for b in bands], *[b[1] for b in bands])


def step_call(kernel, bands, windows, extra, outs, scratch=()):
    n = bands[0][0].shape[0]
    operands = [b[0] for b in bands] + [b[1] for b in bands] + list(windows) + list(extra)
    rows = windows[0].shape[0]
    return pl.pallas_call(
        kernel,
        out_shape=outs,
        compiler_params=vmem_limit(*operands, scratch=32 * rows * n),
        in_specs=[VMEM] * len(operands),
        out_specs=jax.tree.map(lambda _: VMEM, outs),
        scratch_shapes=scratch,
        cost_estimate=pl.CostEstimate(flops=6 * n * n * rows * len(bands), bytes_accessed=4 * n * n * len(bands), transcendentals=0),
    )(*operands)


def on_device(perturbations, probes):
    row_count = lax.axis_size("row")
    col_count = lax.axis_size("col")
    n = perturbations.shape[1]
    state_count = n * col_count
    window = state_count // 4
    reach = col_count // 4
    pairs = reach // 2
    probe_count = probes.shape[1] // row_count
    sides = [(span, late) for late in (0, 1) for span in range(1, pairs + 1)]
    keys = [None] + [(span, late) for span in range(1, pairs + 1) for late in (0, 1)]
    inner_keys = keys[: 2 * pairs - 1]
    last_pair = keys[-2:]

    def window_of(held, outer):
        inner = [core_swap(held[k]) for k in inner_keys]
        return [held[k] for k in keys] + inner + [core_swap(outer)]

    first_ahead = side_sign(last_pair[0]) > 0
    far_first = first_ahead == (device_core() == 0)
    perturbations, first_ahead, far_first = lax.optimization_barrier((perturbations, first_ahead, far_first))

    def far_pick(held):
        return jnp.where(far_first, held[last_pair[0]], held[last_pair[1]])

    def exchange(block):
        return {None: block} | {k: ring_swap(block, k) for k in sides}

    last_mask = row_count - 1
    blocks = {None: {0: perturbations}}
    for k in sides:
        blocks[k] = {0: ring_swap(perturbations, k)}
    for mask in range(last_mask, 0, -1):
        blocks[None][mask] = row_xor(perturbations, mask)
    piece = jax.ShapeDtypeStruct((probe_count, n // row_count), jnp.float32)
    turned = pltpu.VMEM((probes.shape[1], probes.shape[0]), jnp.float32)
    pieces = small_call(split_kernel, [probes], [piece] * row_count, [turned])
    pieces = [pieces[0]] + [row_xor(pieces[mask], mask) for mask in range(1, row_count)]
    w0 = small_call(join_kernel, pieces, jax.ShapeDtypeStruct((probe_count, n), jnp.float32))
    held = exchange(w0)
    windows = window_of(held, far_pick(held))
    for k in sides:
        for mask in range(1, last_mask):
            blocks[k][mask] = row_xor(blocks[k][0], mask)
        blocks[k][last_mask] = ring_swap(blocks[None][last_mask], k)

    def offset_of(key, inner):
        def offset():
            own = 0 if key is None else 2 * key[0] * side_sign(key)
            return own + (1 - 2 * device_core() if inner else 0)

        return offset

    offsets = [offset_of(k, False) for k in keys] + [offset_of(k, True) for k in inner_keys]
    offsets.append(lambda: (1 - reach) * (1 - 2 * device_core()))
    slots = len(offsets)
    bands = {}
    own_pieces = [blocks[None][mask] for mask in range(row_count)]
    high, low, y1, square, *left, normed = gram(None, None, own_pieces, windows[0], None, window)
    bands[0] = (high, low)

    def add_slot(k, pieces, carried, **kinds):
        high, low, *carried = gram(offsets[k], left, pieces, windows[k], carried, window, **kinds)
        bands[k] = (high, low)
        return carried

    def add_side(k, carried):
        return add_slot(keys.index(k), list(blocks[k].values()), carried)

    carried = [y1, square]
    near_block = core_swap(normed)
    far = [core_swap(far_pick({k: blocks[k][mask] for k in sides})) for mask in range(row_count)]
    for k in sides[:pairs]:
        carried = add_side(k, carried)
    for place, k in enumerate(inner_keys):
        slot = len(keys) + place
        if k is None:
            carried = add_slot(slot, [near_block], carried, raw=False)
        else:
            pieces = [core_swap(block) for block in blocks[k].values()]
            carried = add_slot(slot, pieces, carried)
    for k in sides[pairs:]:
        carried = add_side(k, carried)
    y1, _ = add_slot(slots - 1, far, carried, last=True)
    bands = [bands[k] for k in range(slots)]

    localized = skewed(offsets, reach, bands)

    held = exchange(y1)
    windows = window_of(held, far_pick(held))
    second = functools.partial(second_kernel, slots, probe_count, pairs)
    y2 = step_call(second, bands, windows, [], jax.ShapeDtypeStruct(y1.shape, y1.dtype))
    held = exchange(y2)
    row = lax.broadcasted_iota(jnp.int32, y2.shape, 0) - probe_count
    first, second = held[last_pair[0]], held[last_pair[1]]
    tail = jnp.where(row == 0, y2, jnp.where((row == 1) == first_ahead, first, second))
    windows = window_of(held, jnp.where(row < 0, far_pick(held), tail))
    pieces = step_call(
        functools.partial(last_kernel, slots, probe_count, pairs, state_count),
        bands, windows, [w0, y1, y2], [piece] * row_count,
        scratch=[pltpu.VMEM((probe_count, n), jnp.float32)],
    )
    pieces = [pieces[0]] + [row_xor(pieces[mask], mask) for mask in range(1, row_count)]
    sampled = small_call(gather_kernel, pieces, jax.ShapeDtypeStruct(probes.shape, jnp.float32), [turned])
    return (localized, sampled)


def solution(mesh):
    return jax.shard_map(
        on_device,
        mesh=mesh,
        in_specs=(P("row", "col"), P(("col", "row"), None)),
        out_specs=(P("col", "row"), P(("col", "row"), None)),
        check_vma=False,
    )
```

```python
import functools
import math

import jax
import jax.numpy as jnp
from jax import lax
from jax.experimental import pallas as pl
from jax.experimental.pallas import tpu as pltpu
from jax.sharding import PartitionSpec as P


EPSILON = 1e-06
POWER_TERMS = (
    2.0 / math.pi - 4.0 / (3.0 * math.pi) - 4.0 / (15.0 * math.pi) - 4.0 / (35.0 * math.pi),
    8.0 / (3.0 * math.pi) + 32.0 / (15.0 * math.pi) + 72.0 / (35.0 * math.pi),
    -32.0 / (15.0 * math.pi) - 192.0 / (35.0 * math.pi),
    128.0 / (35.0 * math.pi),
)
SUBLANES = 8
LANES = 128
VMEM = pl.BlockSpec(memory_space=pltpu.VMEM)
ANY = pl.BlockSpec(memory_space=pl.ANY)
NN = (((1,), (0,)), ((), ()))
NT = (((1,), (1,)), ((), ()))


def side_sign(side):
    span, late = side
    odd = (lax.axis_index("col") // 2 // span) & 1
    return (1 - 2 * late) * (2 * odd - 1)


def ring_swap(block, side):
    span, late = side
    count = lax.axis_size("col") // 2
    route = []
    for i in range(count):
        ahead = (i // span) % 2 != late
        other = (i + span if ahead else i - span) % count
        route += [(2 * i, 2 * other), (2 * i + 1, 2 * other + 1)]
    return lax.ppermute(block, "col", route)


def core_swap(block):
    return lax.ppermute(block, "col", [(i ^ 1, i) for i in range(lax.axis_size("col"))])


def chip_xor(block, mask):
    return lax.ppermute(block, "col", [(i ^ (2 * mask), i) for i in range(lax.axis_size("col"))])


def row_xor(block, mask):
    return lax.ppermute(block, "row", [(i ^ mask, i) for i in range(lax.axis_size("row"))])


def vmem_limit(*arrays, scratch=0):
    held = sum(math.prod(a.shape) * a.dtype.itemsize for a in arrays) + scratch
    return pltpu.CompilerParams(vmem_limit_bytes=min(held + (4 << 20), 60 << 20))


def split(value):
    high = value.astype(jnp.bfloat16)
    return high, (value - high.astype(jnp.float32)).astype(jnp.bfloat16)


def dot(a, b, dims):
    return lax.dot_general(a, b, dims, preferred_element_type=jnp.float32)


def normalize(pieces, quarter):
    x = jnp.concatenate([p[:quarter, :] for p in pieces], 0)
    centered = x - jnp.sum(x, 0, keepdims=True) / x.shape[0]
    spread = jnp.sqrt(jnp.sum(centered * centered, 0, keepdims=True) + EPSILON)
    return centered * (1.0 / spread)


def device_core():
    return lax.axis_index("col") & 1


def gram_kernel(window, count, members, probes, offset, raw, last, explicit, *refs):
    refs = list(refs)
    take = lambda k: [refs.pop(0) for _ in range(k)]
    own = offset is None
    left_high_ref, left_low_ref = (None, None) if own else take(2)
    pieces = take(count)
    w_ref = take(1)[0] if explicit else pieces[-1].at[pl.ds(members // count, probes), :]
    sum_ref, squares_ref = (None, None) if own else take(2)
    high_ref, low_ref, y_ref, square_ref = take(4)
    normed = normalize(pieces, members // count) if raw else pieces[0][:members, :]
    n = normed.shape[1]
    if own:
        left_high_out, left_low_out, normed_out = take(3)
        normed_out[:members, :] = normed
        normed_out[members:, :] = w_ref[...]
        left_high, left_low = split(normed.T)
        left_high_out[...] = left_high
        left_low_out[...] = left_low
    else:
        left_high, left_low = left_high_ref[...], left_low_ref[...]
    high, low = split(normed)
    part = dot(left_high, high, NN) + dot(left_high, low, NN) + dot(left_low, high, NN)
    ahead = lax.broadcasted_iota(jnp.int32, (n, n), 1) - lax.broadcasted_iota(jnp.int32, (n, n), 0)
    shift = 0 if own else offset() * n
    distance = jnp.abs(ahead + shift).astype(jnp.float32)
    tapered = part * jnp.maximum(0.0, 1.0 - distance * (1.0 / window))
    high, low = split(tapered)
    high_ref[...] = high
    low_ref[...] = low
    square = jnp.sum((tapered * tapered).reshape(n // SUBLANES, SUBLANES, n), 0)
    product = band_product([(high_ref, low_ref)], [w_ref])
    if not own:
        square += squares_ref[...]
        product += sum_ref[...]
    y_ref[...] = product
    if last:
        square = functools.reduce(jnp.add, [square[:, k : k + LANES] for k in range(0, n, LANES)])
    square_ref[...] = square


def gram(offset, left, pieces, w, shape, carried, window, raw=True, last=False):
    own = offset is None
    members, probes, n = shape
    behind = [] if w is None else [w]
    band = jax.ShapeDtypeStruct((n, n), jnp.bfloat16)
    side = jax.ShapeDtypeStruct((n, members), jnp.bfloat16)
    square = jax.ShapeDtypeStruct((SUBLANES, LANES if last else n), jnp.float32)
    outs = [band, band, jax.ShapeDtypeStruct((probes, n), jnp.float32), square]
    if own:
        operands = [*pieces, *behind]
        outs += [side, side, jax.ShapeDtypeStruct((members + probes, n), jnp.float32)]
    else:
        operands = [*left, *pieces, *behind, *carried]
    return pl.pallas_call(
        functools.partial(gram_kernel, window, len(pieces), members, probes, offset, raw, last, w is not None),
        out_shape=tuple(outs),
        compiler_params=vmem_limit(*operands, *outs, scratch=16 * n * (n + members)),
        in_specs=[VMEM] * len(operands),
        out_specs=[VMEM] * len(outs),
        cost_estimate=pl.CostEstimate(flops=6 * n * n * members, bytes_accessed=4 * n * members, transcendentals=0),
    )(*operands)


def band_product(bands, windows):
    probes, n = windows[0].shape
    wide = jnp.zeros((2 * probes, n), jnp.float32)
    narrow = jnp.zeros((probes, n), jnp.float32)
    for (high_ref, low_ref), w_ref in zip(bands, windows):
        high, low = split(w_ref[...])
        band_high = high_ref[...]
        wide += dot(jnp.concatenate([high, low], 0), band_high, NT)
        narrow += dot(high, low_ref[...], NT)
    return wide[:probes] + wide[probes:] + narrow


def unpack(refs, slots):
    bands = list(zip(refs[:slots], refs[slots : 2 * slots]))
    return bands, refs[2 * slots : 3 * slots], refs[3 * slots :]


def step_kernel(slots, follows, *refs):
    bands, windows, rest = unpack(refs, slots)
    product = band_product(bands, windows)
    if follows:
        product += rest[0][...]
    rest[-1][...] = product


def last_kernel(slots, state_count, *refs):
    bands, windows, (sum_ref, square_ref, w0_ref, y1_ref, y2_ref, *out_refs, total_ref) = unpack(refs, slots)
    y3 = band_product(bands, windows) + sum_ref[...]
    squares = jnp.sum(jnp.sum(square_ref[...], 1, keepdims=True), 0, keepdims=True)
    scale = jnp.broadcast_to(squares, (1, y3.shape[1])) / state_count
    total = POWER_TERMS[0] * w0_ref[...]
    total += POWER_TERMS[1] * (y1_ref[...] / scale)
    total += POWER_TERMS[2] * (y2_ref[...] / scale / scale)
    total += POWER_TERMS[3] * (y3 / scale / scale / scale)
    total_ref[...] = jnp.sqrt(scale) * total
    width = out_refs[0].shape[1]
    for mask, out_ref in enumerate(out_refs):
        start = pl.multiple_of((lax.axis_index("row") ^ mask) * width, width)
        out_ref[...] = total_ref[:, pl.ds(start, width)]


def gather_kernel(*refs):
    *piece_refs, out_ref, stack_ref = refs
    height = piece_refs[0].shape[0]
    for mask, piece_ref in enumerate(piece_refs):
        start = pl.multiple_of((lax.axis_index("row") ^ mask) * height, height)
        stack_ref[pl.ds(start, height), :] = piece_ref[...]
    out_ref[...] = stack_ref[...].T


def split_kernel(probes_ref, *refs):
    *piece_refs, stack_ref = refs
    stack_ref[...] = probes_ref[...].T
    height = piece_refs[0].shape[0]
    for mask, piece_ref in enumerate(piece_refs):
        start = pl.multiple_of((lax.axis_index("row") ^ mask) * height, height)
        piece_ref[...] = stack_ref[pl.ds(start, height), :]


def join_kernel(*refs):
    *piece_refs, out_ref = refs
    width = piece_refs[0].shape[1]
    for mask, piece_ref in enumerate(piece_refs):
        start = pl.multiple_of((lax.axis_index("row") ^ mask) * width, width)
        out_ref[:, pl.ds(start, width)] = piece_ref[...]


def small_call(kernel, operands, outs, scratch=()):
    return pl.pallas_call(
        kernel,
        out_shape=outs,
        compiler_params=vmem_limit(*operands, *jax.tree.leaves(outs)),
        in_specs=[VMEM] * len(operands),
        out_specs=jax.tree.map(lambda _: VMEM, outs),
        scratch_shapes=scratch,
    )(*operands)


def skew_kernel(offsets, reach, *refs):
    slots = len(offsets)
    out_ref = refs[2 * slots]
    high_scratch, low_scratch, sem = refs[1 + 2 * slots :]
    n = out_ref.shape[0]
    for place in range(2):
        wanted = lax.axis_index("row") - reach + place
        for k, offset in enumerate(offsets):
            @pl.when(wanted == offset())
            def _(place=place, k=k):
                a = pltpu.make_async_copy(refs[k], high_scratch.at[place], sem.at[0])
                b = pltpu.make_async_copy(refs[slots + k], low_scratch.at[place], sem.at[1])
                a.start()
                b.start()
                a.wait()
                b.wait()

    group = 8
    flip = group - 1 - lax.broadcasted_iota(jnp.int32, (group, n), 0)
    row = lax.broadcasted_iota(jnp.int32, (2 * group, n), 0)
    lane = lax.broadcasted_iota(jnp.int32, (2 * group, n), 1)
    for start in range(0, n, 2 * group):
        rows = slice(start, start + 2 * group)
        near = high_scratch[0, rows, :].astype(jnp.float32) + low_scratch[0, rows, :].astype(jnp.float32)
        far = high_scratch[1, rows, :].astype(jnp.float32) + low_scratch[1, rows, :].astype(jnp.float32)
        value = jnp.where(lane >= row + start, near, far)
        for half in (0, group):
            part = jnp.take_along_axis(value[half : half + group], flip, axis=0)
            part = pltpu.roll(part, (2 * n - start - half - group + 1) % n, 1, stride=1, stride_axis=0)
            out_ref[start + half : start + half + group, :] = jnp.take_along_axis(part, flip, axis=0)


def skewed(offsets, reach, bands):
    slots = len(bands)
    n = bands[0][0].shape[0]
    return pl.pallas_call(
        functools.partial(skew_kernel, offsets, reach),
        out_shape=jax.ShapeDtypeStruct((n, n), jnp.float32),
        in_specs=[ANY] * (2 * slots),
        out_specs=VMEM,
        compiler_params=vmem_limit(scratch=12 * n * n),
        scratch_shapes=[
            pltpu.VMEM((2, n, n), jnp.bfloat16),
            pltpu.VMEM((2, n, n), jnp.bfloat16),
            pltpu.SemaphoreType.DMA((2,)),
        ],
        name="skew_out",
        cost_estimate=pl.CostEstimate(flops=40 * n * n, bytes_accessed=12 * n * n, transcendentals=0),
    )(*[b[0] for b in bands], *[b[1] for b in bands])


def step_call(kernel, bands, windows, extra, outs, scratch=()):
    n = bands[0][0].shape[0]
    operands = [b[0] for b in bands] + [b[1] for b in bands] + list(windows) + list(extra)
    rows = windows[0].shape[0]
    return pl.pallas_call(
        kernel,
        out_shape=outs,
        compiler_params=vmem_limit(*operands, scratch=32 * rows * n),
        in_specs=[VMEM] * len(operands),
        out_specs=jax.tree.map(lambda _: VMEM, outs),
        scratch_shapes=scratch,
        cost_estimate=pl.CostEstimate(flops=6 * n * n * rows * len(bands), bytes_accessed=4 * n * n * len(bands), transcendentals=0),
    )(*operands)


def on_device(perturbations, probes):
    row_count = lax.axis_size("row")
    col_count = lax.axis_size("col")
    n = perturbations.shape[1]
    state_count = n * col_count
    window = state_count // 4
    reach = col_count // 4
    pairs = reach // 2
    probe_count = probes.shape[1] // row_count
    sides = [(span, late) for late in (0, 1) for span in range(1, pairs + 1)]
    keys = [None] + [(span, late) for span in range(1, pairs + 1) for late in (0, 1)]
    inner_keys = keys[: 2 * pairs - 1]
    last_pair = keys[-2:]
    far_first = (side_sign(last_pair[0]) > 0) == (device_core() == 0)
    perturbations, far_first = lax.optimization_barrier((perturbations, far_first))

    def far_pick(held):
        return jnp.where(far_first, held[last_pair[0]], held[last_pair[1]])

    def exchange(block):
        held = {None: block} | {k: ring_swap(block, k) for k in sides}
        inner = [core_swap(held[k]) for k in inner_keys]
        return [held[k] for k in keys] + inner + [core_swap(far_pick(held))]

    piece = jax.ShapeDtypeStruct((probe_count, n // row_count), jnp.float32)
    quarter = perturbations.shape[0]
    members = quarter * row_count
    shape = (members, probe_count, n)
    turned = pltpu.VMEM((probes.shape[1], probes.shape[0]), jnp.float32)
    shares = small_call(split_kernel, [probes], [piece] * row_count, [turned])
    shares = [shares[0]] + [row_xor(shares[mask], mask) for mask in range(1, row_count)]
    w0 = small_call(join_kernel, shares, jax.ShapeDtypeStruct((probe_count, n), jnp.float32))
    w_side = {None: w0} | {k: ring_swap(w0, k) for k in sides}

    last_mask = row_count - 1
    blocks = {None: {0: perturbations}}
    for k in sides:
        blocks[k] = {0: ring_swap(perturbations, k)}
    for mask in range(last_mask, 0, -1):
        blocks[None][mask] = row_xor(perturbations, mask)
    blocks[None] = dict(sorted(blocks[None].items()))
    for k in sides:
        for mask in range(1, last_mask):
            blocks[k][mask] = row_xor(blocks[k][0], mask)
        blocks[k][last_mask] = ring_swap(blocks[None][last_mask], k)

    def offset_of(key, inner):
        def offset():
            own = 0 if key is None else 2 * key[0] * side_sign(key)
            return own + (1 - 2 * device_core() if inner else 0)

        return offset

    offsets = [offset_of(k, False) for k in keys] + [offset_of(k, True) for k in inner_keys]
    offsets.append(lambda: (1 - reach) * (1 - 2 * device_core()))
    slots = len(offsets)
    bands = {}
    own_pieces = list(blocks[None].values())
    high, low, y1, square, *left, normed = gram(None, None, own_pieces, w0, shape, None, window)
    bands[0] = (high, low)

    def add_slot(k, pieces, w, carried, **kinds):
        high, low, *carried = gram(offsets[k], left, pieces, w, shape, carried, window, **kinds)
        bands[k] = (high, low)
        return carried

    def add_side(k, carried):
        return add_slot(keys.index(k), list(blocks[k].values()), w_side[k], carried)

    carried = [y1, square]
    near_block = core_swap(normed)
    far = [far_pick({k: blocks[k][mask] for k in sides}) for mask in range(row_count)]
    far[-1] = jnp.concatenate([far[-1], far_pick(w_side)], 0)
    far = [core_swap(block) for block in far]
    carried = add_slot(len(keys), [near_block], None, carried, raw=False)
    for k in sides:
        carried = add_side(k, carried)
    for place, k in enumerate(inner_keys[1:], 1):
        pieces = [core_swap(block) for block in blocks[k].values()]
        w = core_swap(w_side[k])
        carried = add_slot(len(keys) + place, pieces, w, carried)
    y1, squares = add_slot(slots - 1, far, None, carried, last=True)
    bands = [bands[k] for k in range(slots)]

    localized = skewed(offsets, reach, bands)


    squares += core_swap(squares)
    mask = 1
    while mask < col_count // 2:
        squares += chip_xor(squares, mask)
        mask *= 2

    near = [0, len(keys)]
    beside = list(range(1, len(keys)))
    rest = list(range(len(keys) + 1, slots))

    def advance(block):
        windows = exchange(block)
        pick = lambda items, places: [items[k] for k in places]
        shape = jax.ShapeDtypeStruct(block.shape, block.dtype)
        first = functools.partial(step_kernel, len(near), False)
        total = step_call(first, pick(bands, near), pick(windows, near), [], shape)
        second = functools.partial(step_kernel, len(beside), True)
        total = step_call(second, pick(bands, beside), pick(windows, beside), [total], shape)
        return pick(bands, rest), pick(windows, rest), [total], shape

    *parts, shape = advance(y1)
    y2 = step_call(functools.partial(step_kernel, len(rest), True), *parts, shape)
    far_bands, far_windows, total, shape = advance(y2)
    pieces = step_call(
        functools.partial(last_kernel, len(rest), state_count),
        far_bands, far_windows, total + [squares, w0, y1, y2], [piece] * row_count,
        scratch=[pltpu.VMEM((probe_count, n), jnp.float32)],
    )
    pieces = [pieces[0]] + [row_xor(pieces[mask], mask) for mask in range(1, row_count)]
    sampled = small_call(gather_kernel, pieces, jax.ShapeDtypeStruct(probes.shape, jnp.float32), [turned])
    return (localized, sampled)


def solution(mesh):
    return jax.shard_map(
        on_device,
        mesh=mesh,
        in_specs=(P("row", "col"), P(("col", "row"), None)),
        out_specs=(P("col", "row"), P(("col", "row"), None)),
        check_vma=False,
    )
```

```python
import functools
import math

import jax
import jax.numpy as jnp
from jax import lax
from jax.experimental import pallas as pl
from jax.experimental.pallas import tpu as pltpu
from jax.sharding import PartitionSpec as P


EPSILON = 1e-06
POWER_TERMS = (
    2.0 / math.pi - 4.0 / (3.0 * math.pi) - 4.0 / (15.0 * math.pi) - 4.0 / (35.0 * math.pi),
    8.0 / (3.0 * math.pi) + 32.0 / (15.0 * math.pi) + 72.0 / (35.0 * math.pi),
    -32.0 / (15.0 * math.pi) - 192.0 / (35.0 * math.pi),
    128.0 / (35.0 * math.pi),
)
SUBLANES = 8
LANES = 128
VMEM = pl.BlockSpec(memory_space=pltpu.VMEM)
ANY = pl.BlockSpec(memory_space=pl.ANY)
NN = (((1,), (0,)), ((), ()))
NT = (((1,), (1,)), ((), ()))


def side_sign(side):
    span, late = side
    odd = (lax.axis_index("col") // 2 // span) & 1
    return (1 - 2 * late) * (2 * odd - 1)


def ring_swap(block, side):
    span, late = side
    count = lax.axis_size("col") // 2
    route = []
    for i in range(count):
        ahead = (i // span) % 2 != late
        other = (i + span if ahead else i - span) % count
        route += [(2 * i, 2 * other), (2 * i + 1, 2 * other + 1)]
    return lax.ppermute(block, "col", route)


def core_swap(block):
    return lax.ppermute(block, "col", [(i ^ 1, i) for i in range(lax.axis_size("col"))])


def chip_xor(block, mask):
    return lax.ppermute(block, "col", [(i ^ (2 * mask), i) for i in range(lax.axis_size("col"))])


def row_xor(block, mask):
    return lax.ppermute(block, "row", [(i ^ mask, i) for i in range(lax.axis_size("row"))])


def vmem_limit(*arrays, scratch=0):
    held = sum(math.prod(a.shape) * a.dtype.itemsize for a in arrays) + scratch
    return pltpu.CompilerParams(vmem_limit_bytes=min(held + (4 << 20), 60 << 20))


def split(value):
    high = value.astype(jnp.bfloat16)
    return high, (value - high.astype(jnp.float32)).astype(jnp.bfloat16)


def dot(a, b, dims):
    return lax.dot_general(a, b, dims, preferred_element_type=jnp.float32)


def normalize(pieces, quarter):
    x = jnp.concatenate([p[:quarter, :] for p in pieces], 0)
    centered = x - jnp.sum(x, 0, keepdims=True) / x.shape[0]
    spread = jnp.sqrt(jnp.sum(centered * centered, 0, keepdims=True) + EPSILON)
    return centered * (1.0 / spread)


def device_core():
    return lax.axis_index("col") & 1


def gram_kernel(window, count, members, probes, offset, raw, last, explicit, *refs):
    refs = list(refs)
    take = lambda k: [refs.pop(0) for _ in range(k)]
    own = offset is None
    left_high_ref, left_low_ref = (None, None) if own else take(2)
    pieces = take(count)
    w_ref = take(1)[0] if explicit else pieces[-1].at[pl.ds(members // count, probes), :]
    sum_ref, squares_ref = (None, None) if own else take(2)
    high_ref, low_ref, y_ref, square_ref = take(4)
    normed = normalize(pieces, members // count) if raw else pieces[0][:members, :]
    n = normed.shape[1]
    if own:
        left_high_out, left_low_out, normed_out = take(3)
        normed_out[:members, :] = normed
        normed_out[members:, :] = w_ref[...]
        left_high, left_low = split(normed.T)
        left_high_out[...] = left_high
        left_low_out[...] = left_low
    else:
        left_high, left_low = left_high_ref[...], left_low_ref[...]
    high, low = split(normed)
    part = dot(
        jnp.concatenate([left_high, left_high, left_low], 1), jnp.concatenate([high, low, high], 0), NN
    )
    column = lax.broadcasted_iota(jnp.int32, (1, n), 1)
    row = lax.broadcasted_iota(jnp.int32, (n, 1), 0)
    if own:
        tapered = part * jnp.maximum(0.0, 1.0 - jnp.abs(column - row).astype(jnp.float32) * (1.0 / window))
    else:
        shift = offset()
        sign = jnp.where(shift > 0, 1, -1)
        beyond = 1.0 - (sign * (column + shift * n)).astype(jnp.float32) * (1.0 / window)
        tapered = part * jnp.maximum(0.0, beyond + (sign * row).astype(jnp.float32) * (1.0 / window))
    high, low = split(tapered)
    high_ref[...] = high
    low_ref[...] = low
    square = jnp.sum((tapered * tapered).reshape(n // SUBLANES, SUBLANES, n), 0)
    product = band_product([(high_ref, low_ref)], [w_ref])
    if not own:
        square += squares_ref[...]
        product += sum_ref[...]
    y_ref[...] = product
    if last:
        square = functools.reduce(jnp.add, [square[:, k : k + LANES] for k in range(0, n, LANES)])
    square_ref[...] = square


def gram(offset, left, pieces, w, shape, carried, window, raw=True, last=False):
    own = offset is None
    members, probes, n = shape
    behind = [] if w is None else [w]
    band = jax.ShapeDtypeStruct((n, n), jnp.bfloat16)
    side = jax.ShapeDtypeStruct((n, members), jnp.bfloat16)
    square = jax.ShapeDtypeStruct((SUBLANES, LANES if last else n), jnp.float32)
    outs = [band, band, jax.ShapeDtypeStruct((probes, n), jnp.float32), square]
    if own:
        operands = [*pieces, *behind]
        outs += [side, side, jax.ShapeDtypeStruct((members + probes, n), jnp.float32)]
    else:
        operands = [*left, *pieces, *behind, *carried]
    return pl.pallas_call(
        functools.partial(gram_kernel, window, len(pieces), members, probes, offset, raw, last, w is not None),
        out_shape=tuple(outs),
        compiler_params=vmem_limit(*operands, *outs, scratch=16 * n * (n + members)),
        in_specs=[VMEM] * len(operands),
        out_specs=[VMEM] * len(outs),
        cost_estimate=pl.CostEstimate(flops=6 * n * n * members, bytes_accessed=4 * n * members, transcendentals=0),
    )(*operands)


def band_product(bands, windows):
    probes, n = windows[0].shape
    wide = jnp.zeros((2 * probes, n), jnp.float32)
    narrow = jnp.zeros((probes, n), jnp.float32)
    for (high_ref, low_ref), w_ref in zip(bands, windows):
        high, low = split(w_ref[...])
        band_high = high_ref[...]
        wide += dot(jnp.concatenate([high, low], 0), band_high, NT)
        narrow += dot(high, low_ref[...], NT)
    return wide[:probes] + wide[probes:] + narrow


def unpack(refs, slots):
    bands = list(zip(refs[:slots], refs[slots : 2 * slots]))
    return bands, refs[2 * slots : 3 * slots], refs[3 * slots :]


def step_kernel(slots, follows, *refs):
    bands, windows, rest = unpack(refs, slots)
    product = band_product(bands, windows)
    if follows:
        product += rest[0][...]
    rest[-1][...] = product


def last_kernel(slots, state_count, *refs):
    bands, windows, (sum_ref, square_ref, w0_ref, y1_ref, y2_ref, *out_refs, total_ref) = unpack(refs, slots)
    y3 = band_product(bands, windows) + sum_ref[...]
    squares = jnp.sum(jnp.sum(square_ref[...], 1, keepdims=True), 0, keepdims=True)
    scale = jnp.broadcast_to(squares, (1, y3.shape[1])) / state_count
    total = POWER_TERMS[0] * w0_ref[...]
    total += POWER_TERMS[1] * (y1_ref[...] / scale)
    total += POWER_TERMS[2] * (y2_ref[...] / scale / scale)
    total += POWER_TERMS[3] * (y3 / scale / scale / scale)
    total_ref[...] = jnp.sqrt(scale) * total
    width = out_refs[0].shape[1]
    for mask, out_ref in enumerate(out_refs):
        start = pl.multiple_of((lax.axis_index("row") ^ mask) * width, width)
        out_ref[...] = total_ref[:, pl.ds(start, width)]


def gather_kernel(*refs):
    *piece_refs, out_ref, stack_ref = refs
    height = piece_refs[0].shape[0]
    for mask, piece_ref in enumerate(piece_refs):
        start = pl.multiple_of((lax.axis_index("row") ^ mask) * height, height)
        stack_ref[pl.ds(start, height), :] = piece_ref[...]
    out_ref[...] = stack_ref[...].T


def split_kernel(probes_ref, *refs):
    *piece_refs, stack_ref = refs
    stack_ref[...] = probes_ref[...].T
    height = piece_refs[0].shape[0]
    for mask, piece_ref in enumerate(piece_refs):
        start = pl.multiple_of((lax.axis_index("row") ^ mask) * height, height)
        piece_ref[...] = stack_ref[pl.ds(start, height), :]


def join_kernel(*refs):
    *piece_refs, out_ref = refs
    width = piece_refs[0].shape[1]
    for mask, piece_ref in enumerate(piece_refs):
        start = pl.multiple_of((lax.axis_index("row") ^ mask) * width, width)
        out_ref[:, pl.ds(start, width)] = piece_ref[...]


def small_call(kernel, operands, outs, scratch=()):
    return pl.pallas_call(
        kernel,
        out_shape=outs,
        compiler_params=vmem_limit(*operands, *jax.tree.leaves(outs)),
        in_specs=[VMEM] * len(operands),
        out_specs=jax.tree.map(lambda _: VMEM, outs),
        scratch_shapes=scratch,
    )(*operands)


def skew_kernel(offsets, reach, *refs):
    slots = len(offsets)
    out_ref = refs[2 * slots]
    high_scratch, low_scratch, sem = refs[1 + 2 * slots :]
    n = out_ref.shape[0]
    for place in range(2):
        wanted = lax.axis_index("row") - reach + place
        for k, offset in enumerate(offsets):
            @pl.when(wanted == offset())
            def _(place=place, k=k):
                a = pltpu.make_async_copy(refs[k], high_scratch.at[place], sem.at[0])
                b = pltpu.make_async_copy(refs[slots + k], low_scratch.at[place], sem.at[1])
                a.start()
                b.start()
                a.wait()
                b.wait()

    group = 8
    flip = group - 1 - lax.broadcasted_iota(jnp.int32, (group, n), 0)
    row = lax.broadcasted_iota(jnp.int32, (2 * group, n), 0)
    lane = lax.broadcasted_iota(jnp.int32, (2 * group, n), 1)
    for start in range(0, n, 2 * group):
        rows = slice(start, start + 2 * group)
        near = high_scratch[0, rows, :].astype(jnp.float32) + low_scratch[0, rows, :].astype(jnp.float32)
        far = high_scratch[1, rows, :].astype(jnp.float32) + low_scratch[1, rows, :].astype(jnp.float32)
        value = jnp.where(lane >= row + start, near, far)
        for half in (0, group):
            part = jnp.take_along_axis(value[half : half + group], flip, axis=0)
            part = pltpu.roll(part, (2 * n - start - half - group + 1) % n, 1, stride=1, stride_axis=0)
            out_ref[start + half : start + half + group, :] = jnp.take_along_axis(part, flip, axis=0)


def skewed(offsets, reach, bands):
    slots = len(bands)
    n = bands[0][0].shape[0]
    return pl.pallas_call(
        functools.partial(skew_kernel, offsets, reach),
        out_shape=jax.ShapeDtypeStruct((n, n), jnp.float32),
        in_specs=[ANY] * (2 * slots),
        out_specs=VMEM,
        compiler_params=vmem_limit(scratch=12 * n * n),
        scratch_shapes=[
            pltpu.VMEM((2, n, n), jnp.bfloat16),
            pltpu.VMEM((2, n, n), jnp.bfloat16),
            pltpu.SemaphoreType.DMA((2,)),
        ],
        name="skew_out",
        cost_estimate=pl.CostEstimate(flops=40 * n * n, bytes_accessed=12 * n * n, transcendentals=0),
    )(*[b[0] for b in bands], *[b[1] for b in bands])


def step_call(kernel, bands, windows, extra, outs, scratch=()):
    n = bands[0][0].shape[0]
    operands = [b[0] for b in bands] + [b[1] for b in bands] + list(windows) + list(extra)
    rows = windows[0].shape[0]
    return pl.pallas_call(
        kernel,
        out_shape=outs,
        compiler_params=vmem_limit(*operands, scratch=32 * rows * n),
        in_specs=[VMEM] * len(operands),
        out_specs=jax.tree.map(lambda _: VMEM, outs),
        scratch_shapes=scratch,
        cost_estimate=pl.CostEstimate(flops=6 * n * n * rows * len(bands), bytes_accessed=4 * n * n * len(bands), transcendentals=0),
    )(*operands)


def on_device(perturbations, probes):
    row_count = lax.axis_size("row")
    col_count = lax.axis_size("col")
    n = perturbations.shape[1]
    state_count = n * col_count
    window = state_count // 4
    reach = col_count // 4
    pairs = reach // 2
    probe_count = probes.shape[1] // row_count
    sides = [(span, late) for late in (0, 1) for span in range(1, pairs + 1)]
    keys = [None] + [(span, late) for span in range(1, pairs + 1) for late in (0, 1)]
    inner_keys = keys[: 2 * pairs - 1]
    last_pair = keys[-2:]
    far_first = (side_sign(last_pair[0]) > 0) == (device_core() == 0)
    perturbations, far_first = lax.optimization_barrier((perturbations, far_first))

    def far_pick(held):
        return jnp.where(far_first, held[last_pair[0]], held[last_pair[1]])

    def exchange(block):
        held = {None: block} | {k: ring_swap(block, k) for k in sides}
        inner = [core_swap(held[k]) for k in inner_keys]
        return [held[k] for k in keys] + inner + [core_swap(far_pick(held))]

    piece = jax.ShapeDtypeStruct((probe_count, n // row_count), jnp.float32)
    quarter = perturbations.shape[0]
    members = quarter * row_count
    shape = (members, probe_count, n)
    turned = pltpu.VMEM((probes.shape[1], probes.shape[0]), jnp.float32)
    shares = small_call(split_kernel, [probes], [piece] * row_count, [turned])
    shares = [shares[0]] + [row_xor(shares[mask], mask) for mask in range(1, row_count)]
    w0 = small_call(join_kernel, shares, jax.ShapeDtypeStruct((probe_count, n), jnp.float32))
    w_side = {None: w0} | {k: ring_swap(w0, k) for k in sides}

    last_mask = row_count - 1
    blocks = {None: {0: perturbations}}
    for k in sides:
        blocks[k] = {0: ring_swap(perturbations, k)}
    for mask in range(last_mask, 0, -1):
        blocks[None][mask] = row_xor(perturbations, mask)
    blocks[None] = dict(sorted(blocks[None].items()))
    for k in sides:
        for mask in range(1, last_mask):
            blocks[k][mask] = row_xor(blocks[k][0], mask)
        blocks[k][last_mask] = ring_swap(blocks[None][last_mask], k)

    def offset_of(key, inner):
        def offset():
            own = 0 if key is None else 2 * key[0] * side_sign(key)
            return own + (1 - 2 * device_core() if inner else 0)

        return offset

    offsets = [offset_of(k, False) for k in keys] + [offset_of(k, True) for k in inner_keys]
    offsets.append(lambda: (1 - reach) * (1 - 2 * device_core()))
    slots = len(offsets)
    bands = {}
    own_pieces = list(blocks[None].values())
    high, low, y1, square, *left, normed = gram(None, None, own_pieces, w0, shape, None, window)
    bands[0] = (high, low)

    def add_slot(k, pieces, w, carried, **kinds):
        high, low, *carried = gram(offsets[k], left, pieces, w, shape, carried, window, **kinds)
        bands[k] = (high, low)
        return carried

    def add_side(k, carried):
        return add_slot(keys.index(k), list(blocks[k].values()), w_side[k], carried)

    carried = [y1, square]
    near_block = core_swap(normed)
    far = [far_pick({k: blocks[k][mask] for k in sides}) for mask in range(row_count)]
    far[-1] = jnp.concatenate([far[-1], far_pick(w_side)], 0)
    far = [core_swap(block) for block in far]
    carried = add_slot(len(keys), [near_block], None, carried, raw=False)
    for k in sides:
        carried = add_side(k, carried)
    for place, k in enumerate(inner_keys[1:], 1):
        pieces = [core_swap(block) for block in blocks[k].values()]
        w = core_swap(w_side[k])
        carried = add_slot(len(keys) + place, pieces, w, carried)
    y1, squares = add_slot(slots - 1, far, None, carried, last=True)
    bands = [bands[k] for k in range(slots)]

    localized = skewed(offsets, reach, bands)


    squares += core_swap(squares)
    mask = 1
    while mask < col_count // 2:
        squares += chip_xor(squares, mask)
        mask *= 2

    near = [0, len(keys)]
    beside = list(range(1, len(keys)))
    rest = list(range(len(keys) + 1, slots))

    def advance(block):
        windows = exchange(block)
        pick = lambda items, places: [items[k] for k in places]
        shape = jax.ShapeDtypeStruct(block.shape, block.dtype)
        first = functools.partial(step_kernel, len(near), False)
        total = step_call(first, pick(bands, near), pick(windows, near), [], shape)
        second = functools.partial(step_kernel, len(beside), True)
        total = step_call(second, pick(bands, beside), pick(windows, beside), [total], shape)
        return pick(bands, rest), pick(windows, rest), [total], shape

    *parts, shape = advance(y1)
    y2 = step_call(functools.partial(step_kernel, len(rest), True), *parts, shape)
    far_bands, far_windows, total, shape = advance(y2)
    pieces = step_call(
        functools.partial(last_kernel, len(rest), state_count),
        far_bands, far_windows, total + [squares, w0, y1, y2], [piece] * row_count,
        scratch=[pltpu.VMEM((probe_count, n), jnp.float32)],
    )
    pieces = [pieces[0]] + [row_xor(pieces[mask], mask) for mask in range(1, row_count)]
    sampled = small_call(gather_kernel, pieces, jax.ShapeDtypeStruct(probes.shape, jnp.float32), [turned])
    return (localized, sampled)


def solution(mesh):
    return jax.shard_map(
        on_device,
        mesh=mesh,
        in_specs=(P("row", "col"), P(("col", "row"), None)),
        out_specs=(P("col", "row"), P(("col", "row"), None)),
        check_vma=False,
    )
```
